512 devices in a mesh: band: 32 (over z_lo, y), member: 16 (over x, z_hi, core).
Axes of the slice: x: 4, y: 8, z: 8 (z_hi: 2, z_lo: 4; z = z_hi * 4 + z_lo), core: 2. Of those that a mesh axis runs over, the one named last changes fastest.
Arguments:
- targets: float32 [512, 64, 4096], P(('band', 'member')), may hold values from -6 to 6
- sources: float32 [64, 64, 4096], P('band', 'member'), may hold values from -6 to 6
Outputs:
- exchange: float32 [512, 64, 4096], P(('band', 'member'))
The draws below stay inside these ranges and needn't reach their ends.
All inputs are finite; a program needn't handle non-finite values.
Results may differ from the reference program's by a relative error of at most 0.0003.
Values sent between devices are 32-bit elements; how exact they have to be, the bound alone decides.
A program may use at most 64 MiB of HBM per device.

```python
import jax
import jax.numpy as jnp
from jax import lax

G = 64
TGT_DEV = 1
SRC_BLOCK = 2
STOPS = 2
TARGETS = 512
SOURCES = 64
N_BAND = 32
N_MEMBER = 16


def level_of(key, extent, shards, least, largest):
    level = 1.0
    for position, parts in shards:
        heights = jax.random.uniform(jax.random.fold_in(jax.random.fold_in(key, 6), position), (parts,), jnp.float32, least / len(shards), largest / len(shards))
        level = level * jnp.repeat(jnp.exp(heights), extent[position] // parts).reshape((-1,) + (1,) * (len(extent) - 1 - position))
    return level


def centred(own_key, extent, scale, limit, shards=(), kind=jnp.bfloat16):
    loudness = level_of(own_key, extent, shards, -0.22, 0.18) if shards else 1.0
    values = jax.random.normal(own_key, extent, jnp.float32) * scale * loudness
    return jnp.minimum(jnp.maximum(values, -limit), limit).astype(kind)


def setup_inputs(seed: int = 0) -> dict:
    key_of = jax.random.split(jax.random.key(seed), 3)
    return {
        "targets": centred(key_of[0], (TARGETS, G, G * G), 1.0, 6.0, ((0, 512),), jnp.float32),
        "sources": centred(key_of[1], (SOURCES, G, G * G), 1.0, 6.0, ((0, 32), (1, 16)), jnp.float32),
    }


def sine_axis(field, axis):
    moved = jnp.moveaxis(field, axis, -1)
    count = moved.shape[-1]
    edge = jnp.zeros(moved.shape[:-1] + (1,), moved.dtype)
    extended = jnp.concatenate([edge, moved, edge, -moved[..., ::-1]], axis=-1)
    spectrum = jnp.fft.rfft(extended, axis=-1)
    result = (-0.5 * jnp.imag(spectrum[..., 1:count + 1])).astype(moved.dtype)
    return jnp.moveaxis(result, -1, axis)


def sine_three(field):
    for axis in range(3):
        field = sine_axis(field, axis)
    return field


def inverse_table(dtype):
    wave = jnp.arange(G, dtype=dtype) + 1.0
    single = 4.0 * jnp.sin(jnp.pi * wave / (2.0 * (G + 1))) ** 2
    eigen = single[:, None, None] + single[None, :, None] + single[None, None, :]
    return (2.0 / (G + 1)) ** 3 / eigen


def reference(targets, sources):
    group = N_MEMBER * TGT_DEV
    inverse_eigen = inverse_table(targets.dtype)
    bands = (jnp.arange(TARGETS) // group).astype(jnp.int32)

    def one_target(item):
        target, band = item
        cube = target.reshape(G, G, G)
        total = jnp.zeros((G, G, G), targets.dtype)
        for stop in range(STOPS):
            block = ((band - stop) % N_BAND).astype(jnp.int32)
            chosen = lax.dynamic_slice_in_dim(sources, (block * SRC_BLOCK).astype(jnp.int32), SRC_BLOCK, 0)
            for member in range(SRC_BLOCK):
                source = chosen[member].reshape(G, G, G)
                potential = sine_three(sine_three(cube * source) * inverse_eigen)
                total = total - source * potential
        return total.reshape(G, G * G)

    return lax.map(one_target, (targets, bands))
```

```python
import numpy as np
import jax
import jax.numpy as jnp
from jax import lax
from jax.experimental import pallas as pl
from jax.experimental.pallas import tpu as pltpu
from jax.sharding import PartitionSpec as P

bf16 = jnp.bfloat16
f32 = jnp.float32
MESH = pl.DeviceIdType.MESH
UNITS = 4


def split_table(table):
    high = np.asarray(table, np.float32).astype(bf16)
    low = (table - high.astype(np.float64)).astype(np.float32).astype(bf16)
    return high, low


def tables():
    wave = np.arange(64) + 1.0
    sine = np.sin(np.pi * np.outer(wave, wave) / 65)
    single = 4 * np.sin(np.pi * wave / 130) ** 2
    high, low = split_table(np.kron(np.eye(2), sine))
    right = np.block([[high, low], [high, low]])
    plane = np.broadcast_to(np.arange(64).reshape(16, 1, 4), (16, 2, 4)).reshape(-1)
    block = np.broadcast_to(np.arange(2).reshape(1, 2, 1), (16, 2, 4)).reshape(-1)
    out_wave, out_block = np.tile(np.arange(64), 2), np.repeat(np.arange(2), 64)
    left = sine[out_wave][:, plane] * (out_block[:, None] == block[None, :])
    high, low = split_table(left)
    forward = np.block([[high, high], [low, low]])
    high, low = split_table(left.T)
    backward = np.block([[high, high], [low, low]])
    middle = []
    for parity in range(2):
        one = np.kron(sine[parity::2, :32], np.eye(8))
        for matrix in (one, one.T):
            high, low = split_table(matrix)
            middle.append(np.concatenate([high, low], axis=1))
    middle = np.stack(middle).reshape(2, 2, 256, 512)
    sizes = (2, 2, 32, 8, 2, 2, 64)
    par, pair, m, s, bit, top, k3 = np.meshgrid(*[np.arange(n) for n in sizes], indexing="ij")
    k1, k2 = 32 * top + 8 * (2 * pair + bit) + s, 2 * m + par
    inverse = (2.0 / 65) ** 3 / (single[k1] + single[k2] + single[k3])
    return right, forward, backward, middle, inverse.reshape(2, 2, 256, 256).astype(np.float32)


def split(x):
    high = x.astype(bf16)
    return high, (x - high.astype(f32)).astype(bf16)


def dot(a, b):
    return jnp.dot(a, b, preferred_element_type=f32)


def exchange(a, b, low):
    return jnp.where(low, a, pltpu.roll(b, 64, 1)), jnp.where(low, pltpu.roll(a, 64, 1), b)


def forward_block(u, t, s, right, forward, wide):
    low = lax.broadcasted_iota(jnp.int32, (32, 128), 1) < 64
    d = jnp.concatenate([(t[:, v] * s[:, v]).reshape(128, 128) for v in (u, 15 - u)], axis=0)
    dh, dl = split(d)
    y = dot(jnp.concatenate([dh, dl], axis=1), right[...])
    y = y[:, :128] + y[:, 128:]
    w = [jnp.concatenate([q[:128], q[128:]], axis=1) for q in split(y)]
    z = dot(forward[...], jnp.concatenate(w, axis=0))
    z = z[:128] + z[128:]
    x = {}
    for side in range(2):
        lanes = slice(128 * side, 128 * side + 128)
        for l in range(2):
            a, b = z[64 * l : 64 * l + 32, lanes], z[64 * l + 32 : 64 * l + 64, lanes]
            x[side, l, 0], x[side, l, 1] = exchange(a, b, low)
    pairs = [(x[0, l, i], x[1, 1 - l, 1 - i]) for l in range(2) for i in range(2)]
    start = pl.multiple_of(u * 32, 32)
    for parity, parts in ((0, [a + b for a, b in pairs]), (1, [a - b for a, b in pairs])):
        for g in range(4):
            lanes = slice(128 * (g % 2), 128 * (g % 2) + 128)
            high, rest = split(jnp.concatenate([q[8 * g : 8 * g + 8] for q in parts], axis=0))
            wide[parity, g // 2, pl.ds(start, 32), lanes] = high
            wide[parity, g // 2, pl.ds(256 + start, 32), lanes] = rest


def middle_block(parity, pair, wide, middle, inverse, back):
    def times(way, high, low):
        w = middle[parity, way]
        sides = jnp.concatenate([w[:, :256], w], axis=1)
        return dot(sides, jnp.concatenate([high, low, high], axis=0))

    e = wide[parity, pair]
    q = times(0, e[:256], e[256:]) * inverse[parity, pair]
    back[parity, pair] = times(1, *split(q))


def backward_block(u, s, back, right, backward, out, first):
    low = lax.broadcasted_iota(jnp.int32, (32, 128), 1) < 64
    start = pl.multiple_of(u * 32, 32)
    total, differ = [[] for _ in range(4)], [[] for _ in range(4)]
    for g in range(4):
        lanes = slice(128 * (g % 2), 128 * (g % 2) + 128)
        even, odd = (back[p, g // 2, pl.ds(start, 32), lanes] for p in range(2))
        plus, minus = even + odd, even - odd
        for a in range(4):
            total[a].append(plus[8 * a : 8 * a + 8])
            differ[a].append(minus[8 * a : 8 * a + 8])
    total = [jnp.concatenate(q, axis=0) for q in total]
    differ = [jnp.concatenate(q, axis=0) for q in differ][::-1]
    z = []
    for side in (total, differ):
        z.append(jnp.concatenate([*exchange(side[0], side[1], low), *exchange(side[2], side[3], low)], axis=0))
    y = dot(backward[...], jnp.concatenate(split(jnp.concatenate(z, axis=1)), axis=0))
    y = y[:128] + y[128:]
    y = jnp.concatenate([y[:, :128], y[:, 128:]], axis=0)
    q = dot(jnp.concatenate(split(y), axis=1), right[...])
    q = q[:, :128] + q[:, 128:]
    for side, v in ((0, u), (1, 15 - u)):
        term = s[:, v] * q[128 * side : 128 * side + 128].reshape(16, 8, 128)
        out[:, v] = -term if first else out[:, v] - term


def swap_in(src, dst):
    top = lax.broadcasted_iota(jnp.int32, (8, 128), 0) < 4

    def step(v, carry):
        for i in range(8):
            a, b = src[2 * v, 8 * i : 8 * i + 8], src[2 * v + 1, 8 * i : 8 * i + 8]
            dst[2 * i, v] = jnp.where(top, a, pltpu.roll(b, 4, 0))
            dst[2 * i + 1, v] = jnp.where(top, pltpu.roll(a, 4, 0), b)
        return carry

    lax.fori_loop(0, 16, step, 0)


def swap_out(src, dst):
    top = lax.broadcasted_iota(jnp.int32, (8, 128), 0) < 4

    def step(v, carry):
        for i in range(8):
            a, b = src[2 * i, v], src[2 * i + 1, v]
            dst[2 * v, 8 * i : 8 * i + 8] = jnp.where(top, a, pltpu.roll(b, 4, 0))
            dst[2 * v + 1, 8 * i : 8 * i + 8] = jnp.where(top, pltpu.roll(a, 4, 0), b)
        return carry

    lax.fori_loop(0, 16, step, 0)


def kernel(
    target_hbm, source_hbm, right_hbm, forward_hbm, backward_hbm, middle_hbm, inverse_hbm,
    out_hbm,
    target_in, t, acc, s, wide, back, right, forward, backward, middle, inverse,
    send_sem, recv_sem, own_sem, table_sem, target_sem, out_sem,
):
    band, m = lax.axis_index("band"), lax.axis_index("member")
    bands = lax.axis_size("band")
    x, hi, core = m // 4, (m // 2) % 2, m % 2
    index = lambda x, hi, core: x * 4 + hi * 2 + core
    left, right_x, across = (x + 3) % 4, (x + 1) % 4, (x + 2) % 4
    to_sibling = {"member": index(x, hi, 1 - core)}
    to_z = {"member": index(x, 1 - hi, core)}
    to_left = {"member": index(left, hi, core)}
    to_right = {"member": index(right_x, hi, core)}
    to_next = {"band": (band + 1) % bands}
    to_prev = {"band": (band + bands - 1) % bands}

    barrier = pltpu.get_barrier_semaphore()
    for who in (to_z, to_left, to_right, to_next, to_prev, to_sibling):
        pl.semaphore_signal(barrier, inc=1, device_id=who, device_id_type=MESH)

    loads = [
        pltpu.make_async_copy(a, b, table_sem.at[i])
        for i, (a, b) in enumerate(
            ((right_hbm, right), (forward_hbm, forward), (backward_hbm, backward),
             (middle_hbm, middle), (inverse_hbm, inverse))
        )
    ]
    tiles = [
        pltpu.make_async_copy(target_hbm.at[0, :, pl.ds(128 * i, 128)], target_in.at[i], target_sem.at[i])
        for i in range(32)
    ]
    own = [pltpu.make_async_copy(source_hbm.at[k], s.at[k, m], own_sem.at[k]) for k in range(2)]
    for copy in (*own, *tiles, *loads):
        copy.start()

    started = []

    def send(k, slab, slot, who, src=None, unit=None):
        dst_unit = k if unit is None else unit
        copy = pltpu.make_async_remote_copy(
            src_ref=s.at[k, slab] if src is None else src,
            dst_ref=s.at[dst_unit, slab],
            send_sem=send_sem.at[k, slot],
            recv_sem=recv_sem.at[dst_unit, slab],
            device_id=who,
            device_id_type=MESH,
        )
        copy.start()
        started.append(copy)

    def arrived(k, slab):
        pltpu.make_async_remote_copy(
            src_ref=s.at[k, slab], dst_ref=s.at[k, slab],
            send_sem=send_sem.at[k, 0], recv_sem=recv_sem.at[k, slab],
            device_id=to_sibling, device_id_type=MESH,
        ).wait_recv()

    mz = index(x, 1 - hi, core)
    ml, mlz = index(left, hi, core), index(left, 1 - hi, core)
    mr, mrz = index(right_x, hi, core), index(right_x, 1 - hi, core)
    mo, moz = index(across, hi, core), index(across, 1 - hi, core)

    def stage_a(k):
        src = source_hbm.at[k] if k < 2 else None
        if k >= 2:
            arrived(k, m)
        send(k, m, 0, to_z, src)
        send(k, m, 1, to_left, src)
        send(k, m, 2, to_right, src)
        send(k, m, 3, to_sibling, src)

    def stage_b(k):
        arrived(k, mz)
        send(k, mz, 4, to_left)
        send(k, mz, 5, to_right)
        send(k, mz, 6, to_sibling)

    def stage_c(k):
        arrived(k, ml)
        send(k, ml, 7, to_right)
        send(k, ml, 8, to_sibling)
        arrived(k, mr)
        send(k, mr, 9, to_sibling)

    def stage_d(k):
        arrived(k, mrz)
        send(k, mrz, 10, to_left)
        send(k, mrz, 11, to_sibling)
        arrived(k, mlz)
        send(k, mlz, 12, to_sibling)

    def stage_e(k):
        arrived(k, mo)
        send(k, mo, 13, to_sibling)
        arrived(k, moz)
        send(k, moz, 14, to_sibling)

    def stage_f(k):
        for xx in range(4):
            for h in range(2):
                arrived(k, index(xx, h, 1 - core))
        if k < 2:
            own[k].wait()

    def first(k):
        lax.fori_loop(0, 8, lambda u, c: (forward_block(u, t, s.at[k], right, forward, wide), c)[1], 0, unroll=4)

    def second(k):
        lax.fori_loop(0, 4, lambda i, c: (middle_block(i // 2, i % 2, wide, middle, inverse, back), c)[1], 0, unroll=4)

    def third(k):
        lax.fori_loop(0, 8, lambda u, c: (backward_block(u, s.at[k], back, right, backward, acc, k == 0), c)[1], 0, unroll=4)

    pl.semaphore_wait(barrier, 6)
    stage_a(0)
    stage_a(1)
    for k in (2, 3):
        send(k, m, 15, to_next, source_hbm.at[k - 2])
    for copy in tiles:
        copy.wait()
    swap_in(target_in, t)
    for copy in loads:
        copy.wait()
    stage_b(0)
    stage_c(0)
    stage_a(2)
    stage_d(0)
    stage_b(1)
    stage_e(0)
    stage_c(1)
    stage_f(0)
    first(0)
    stage_d(1)
    stage_a(3)
    second(0)
    stage_b(2)
    stage_e(1)
    third(0)
    stage_c(2)
    stage_f(1)
    first(1)
    stage_d(2)
    second(1)
    stage_b(3)
    stage_e(2)
    third(1)
    stage_c(3)
    stage_f(2)
    first(2)
    stage_d(3)
    second(2)
    stage_e(3)
    third(2)
    stage_f(3)
    first(3)
    second(3)
    third(3)
    swap_out(acc, target_in)
    outs = [
        pltpu.make_async_copy(target_in.at[i], out_hbm.at[0, :, pl.ds(128 * i, 128)], out_sem.at[i])
        for i in range(32)
    ]
    for copy in outs:
        copy.start()
    for copy in started:
        copy.wait_send()
    for copy in outs:
        copy.wait()


def body(targets, sources):
    constants = [jnp.asarray(a) for a in tables()]
    slabs = sources.reshape(2, 4, 32, 128).transpose(0, 2, 1, 3).reshape(2, 16, 8, 128)
    anywhere = pl.BlockSpec(memory_space=pl.ANY)
    vmem, dma = pltpu.VMEM, pltpu.SemaphoreType.DMA
    return pl.pallas_call(
        kernel,
        out_shape=jax.ShapeDtypeStruct((1, 64, 4096), f32),
        in_specs=[anywhere] * 7,
        out_specs=anywhere,
        scratch_shapes=[
            vmem((32, 64, 128), f32), vmem((16, 16, 8, 128), f32), vmem((16, 16, 8, 128), f32),
            vmem((UNITS, 16, 16, 8, 128), f32),
            vmem((2, 2, 512, 256), bf16), vmem((2, 2, 256, 256), f32),
            *[vmem(a.shape, a.dtype) for a in constants],
            dma((UNITS, 16)), dma((UNITS, 16)), dma((2,)), dma((5,)), dma((32,)), dma((32,)),
        ],
        compiler_params=pltpu.CompilerParams(
            collective_id=0, has_side_effects=True, vmem_limit_bytes=56 * 2**20
        ),
        name="exchange",
    )(targets, slabs, *constants)


def solution(mesh):
    return jax.shard_map(
        body,
        mesh=mesh,
        in_specs=(P(("band", "member"), None, None), P("band", "member", None)),
        out_specs=P(("band", "member"), None, None),
        check_vma=False,
    )
```

```python
import numpy as np
import jax
import jax.numpy as jnp
from jax import lax
from jax.experimental import pallas as pl
from jax.experimental.pallas import tpu as pltpu
from jax.sharding import PartitionSpec as P

bf16 = jnp.bfloat16
f32 = jnp.float32
MESH = pl.DeviceIdType.MESH
UNITS = 4


def split_table(table):
    high = np.asarray(table, np.float32).astype(bf16)
    low = (table - high.astype(np.float64)).astype(np.float32).astype(bf16)
    return high, low


def tables():
    wave = np.arange(64) + 1.0
    sine = np.sin(np.pi * np.outer(wave, wave) / 65)
    single = 4 * np.sin(np.pi * wave / 130) ** 2
    high, low = split_table(np.kron(np.eye(2), sine))
    right = np.block([[high, low], [high, low]])
    plane = np.broadcast_to(np.arange(64).reshape(16, 1, 4), (16, 2, 4)).reshape(-1)
    block = np.broadcast_to(np.arange(2).reshape(1, 2, 1), (16, 2, 4)).reshape(-1)
    out_wave, out_block = np.tile(np.arange(64), 2), np.repeat(np.arange(2), 64)
    left = sine[out_wave][:, plane] * (out_block[:, None] == block[None, :])
    high, low = split_table(left)
    forward = np.block([[high, high], [low, low]])
    high, low = split_table(left.T)
    backward = np.block([[high, high], [low, low]])
    middle = []
    for parity in range(2):
        one = np.kron(sine[parity::2, :32], np.eye(8))
        for matrix in (one, one.T):
            high, low = split_table(matrix)
            middle.append(np.concatenate([high, low], axis=1))
    middle = np.stack(middle).reshape(2, 2, 256, 512)
    pair, low3, bit, top, k3 = np.meshgrid(*[np.arange(n) for n in (2, 8, 2, 2, 64)], indexing="ij")
    lanes = single[32 * top + 8 * (2 * pair + bit) + low3] + single[k3]
    lanes = lanes.reshape(2, 8, 256).astype(np.float32)
    rows = np.repeat(single[:, None], 256, axis=1).astype(np.float32)
    return right, forward, backward, middle, lanes, rows


def split(x):
    high = x.astype(bf16)
    return high, (x - high.astype(f32)).astype(bf16)


def dot(a, b):
    return jnp.dot(a, b, preferred_element_type=f32)


def exchange(a, b, low):
    return jnp.where(low, a, pltpu.roll(b, 64, 1)), jnp.where(low, pltpu.roll(a, 64, 1), b)


def forward_block(u, t, s, right, forward, wide):
    low = lax.broadcasted_iota(jnp.int32, (32, 128), 1) < 64
    d = jnp.concatenate([(t[:, v] * s[:, v]).reshape(128, 128) for v in (u, 15 - u)], axis=0)
    dh, dl = split(d)
    y = dot(jnp.concatenate([dh, dl], axis=1), right[...])
    y = y[:, :128] + y[:, 128:]
    w = [jnp.concatenate([q[:128], q[128:]], axis=1) for q in split(y)]
    z = dot(forward[...], jnp.concatenate(w, axis=0))
    z = z[:128] + z[128:]
    x = {}
    for side in range(2):
        lanes = slice(128 * side, 128 * side + 128)
        for l in range(2):
            a, b = z[64 * l : 64 * l + 32, lanes], z[64 * l + 32 : 64 * l + 64, lanes]
            x[side, l, 0], x[side, l, 1] = exchange(a, b, low)
    pairs = [(x[0, l, i], x[1, 1 - l, 1 - i]) for l in range(2) for i in range(2)]
    start = pl.multiple_of(u * 32, 32)
    for parity, parts in ((0, [a + b for a, b in pairs]), (1, [a - b for a, b in pairs])):
        for g in range(4):
            lanes = slice(128 * (g % 2), 128 * (g % 2) + 128)
            high, rest = split(jnp.concatenate([q[8 * g : 8 * g + 8] for q in parts], axis=0))
            wide[parity, g // 2, pl.ds(start, 32), lanes] = high
            wide[parity, g // 2, pl.ds(256 + start, 32), lanes] = rest


def middle_block(parity, pair, wide, middle, inverse, back):
    def times(way, high, low):
        w = middle[parity, way]
        sides = jnp.concatenate([w[:, :256], w], axis=1)
        return dot(sides, jnp.concatenate([high, low, high], axis=0))

    e = wide[parity, pair]
    q = times(0, e[:256], e[256:]) * inverse[parity, pair]
    back[parity, pair] = times(1, *split(q))


def backward_block(u, s, back, right, backward, out, first, emit=None):
    low = lax.broadcasted_iota(jnp.int32, (32, 128), 1) < 64
    start = pl.multiple_of(u * 32, 32)
    total, differ = [[] for _ in range(4)], [[] for _ in range(4)]
    for g in range(4):
        lanes = slice(128 * (g % 2), 128 * (g % 2) + 128)
        even, odd = (back[p, g // 2, pl.ds(start, 32), lanes] for p in range(2))
        plus, minus = even + odd, even - odd
        for a in range(4):
            total[a].append(plus[8 * a : 8 * a + 8])
            differ[a].append(minus[8 * a : 8 * a + 8])
    total = [jnp.concatenate(q, axis=0) for q in total]
    differ = [jnp.concatenate(q, axis=0) for q in differ][::-1]
    z = []
    for side in (total, differ):
        z.append(jnp.concatenate([*exchange(side[0], side[1], low), *exchange(side[2], side[3], low)], axis=0))
    y = dot(backward[...], jnp.concatenate(split(jnp.concatenate(z, axis=1)), axis=0))
    y = y[:128] + y[128:]
    y = jnp.concatenate([y[:, :128], y[:, 128:]], axis=0)
    q = dot(jnp.concatenate(split(y), axis=1), right[...])
    q = q[:, :128] + q[:, 128:]
    for side, v in ((0, u), (1, 15 - u)):
        term = s[:, v] * q[128 * side : 128 * side + 128].reshape(16, 8, 128)
        if emit is None:
            out[:, v] = -term if first else out[:, v] - term
        else:
            emit(v, out[:, v] - term)


def swap_in(src, dst):
    top = lax.broadcasted_iota(jnp.int32, (8, 128), 0) < 4

    def step(v, carry):
        for i in range(8):
            a, b = src[2 * v, 8 * i : 8 * i + 8], src[2 * v + 1, 8 * i : 8 * i + 8]
            dst[2 * i, v] = jnp.where(top, a, pltpu.roll(b, 4, 0))
            dst[2 * i + 1, v] = jnp.where(top, pltpu.roll(a, 4, 0), b)
        return carry

    lax.fori_loop(0, 16, step, 0)


def swapped(value):
    top = lax.broadcasted_iota(jnp.int32, (8, 8, 128), 1) < 4
    value = value.reshape(8, 2, 8, 128)
    a, b = value[:, 0], value[:, 1]
    one, two = jnp.where(top, a, pltpu.roll(b, 4, 1)), jnp.where(top, pltpu.roll(a, 4, 1), b)
    return one.reshape(64, 128), two.reshape(64, 128)


def fill_inverse(lanes, rows, inverse):
    factor = (2.0 / 65) ** 3

    def step(m, carry):
        start = pl.multiple_of(8 * m, 8)
        for parity in range(2):
            for pair in range(2):
                eigen = lanes[pair] + rows[pl.ds(2 * m + parity, 1), :]
                inverse[parity, pair, pl.ds(start, 8), :] = factor / eigen
        return carry

    lax.fori_loop(0, 32, step, 0)


def kernel(
    target_hbm, source_hbm, right_hbm, forward_hbm, backward_hbm, middle_hbm, lanes_hbm, rows_hbm,
    out_hbm,
    tiles, t, acc, s, wide, back, inverse, right, forward, backward, middle, lanes, rows,
    link_sem, pass_sem, recv_sem, sibling_sem, own_sem, table_sem, target_sem, out_sem,
):
    band, m = lax.axis_index("band"), lax.axis_index("member")
    bands = lax.axis_size("band")
    columns = bands // 4
    row, column = band // columns, band % columns
    x, hi, core = m // 4, (m // 2) % 2, m % 2
    index = lambda x, hi, core: x * 4 + hi * 2 + core
    left, right_x, across = (x + 3) % 4, (x + 1) % 4, (x + 2) % 4
    to_flip = jnp.where((row == 3) & (column == columns - 1), 1, 0)
    from_flip = jnp.where((row == 0) & (column == 0), 1, 0)
    near = (hi + from_flip) % 2
    to_sibling = {"member": index(x, hi, 1 - core)}
    to_z = {"member": index(x, 1 - hi, core)}
    to_left, to_right = ({"member": index(xx, hi, core)} for xx in (left, right_x))
    to_next = {"band": (band + 1) % bands, "member": index(x, (hi + to_flip) % 2, core)}
    to_prev = {"band": (band + bands - 1) % bands, "member": index(x, near, core)}

    barrier = pltpu.get_barrier_semaphore()
    for who in (to_z, to_left, to_right, to_next, to_prev, to_sibling):
        pl.semaphore_signal(barrier, inc=1, device_id=who, device_id_type=MESH)

    loads = [
        pltpu.make_async_copy(a, b, table_sem.at[i])
        for i, (a, b) in enumerate(
            ((right_hbm, right), (forward_hbm, forward), (backward_hbm, backward),
             (middle_hbm, middle), (lanes_hbm, lanes), (rows_hbm, rows))
        )
    ]
    own = [pltpu.make_async_copy(source_hbm.at[k], s.at[k, m], own_sem.at[k]) for k in range(2)]
    for copy in (*own, *loads):
        copy.start()
    for i in range(32):
        pltpu.make_async_copy(target_hbm.at[0, :, pl.ds(128 * i, 128)], tiles.at[i], target_sem).start()

    def remote(k, slab, piece, who, src, unit):
        window = pl.ds(8 * piece, 8)
        return pltpu.make_async_remote_copy(
            src_ref=s.at[unit, slab, window] if src is None else src.at[window],
            dst_ref=s.at[k, slab, window],
            send_sem=link_sem.at[unit],
            recv_sem=recv_sem.at[k, slab, piece],
            device_id=who,
            device_id_type=MESH,
        )

    def send(k, slab, piece, who, src=None, unit=None):
        remote(k, slab, piece, who, src, k if unit is None else unit).start()

    def arrived(k, slab, piece):
        remote(k, slab, piece, to_left, None, k).wait_recv()

    def share(k, slab, src=None):
        pltpu.make_async_remote_copy(
            src_ref=s.at[k, slab] if src is None else src,
            dst_ref=s.at[k, slab],
            send_sem=pass_sem.at[k],
            recv_sem=sibling_sem.at[k],
            device_id=to_sibling,
            device_id_type=MESH,
        ).start()

    def group(k, count, send_sem, recv_sem):
        block = s.at[k, pl.ds(0, count)]
        return pltpu.make_async_remote_copy(
            src_ref=block, dst_ref=block, send_sem=send_sem, recv_sem=recv_sem,
            device_id=to_sibling, device_id_type=MESH,
        )

    mine, other = index(x, hi, core), index(x, 1 - hi, core)
    halves = range(2)

    def other_out(k):
        for piece in halves:
            arrived(k, other, piece)
            for who in (to_left, to_right):
                send(k, other, piece, who)
        for piece in halves:
            send(k + 2, other, piece, to_next, unit=k)
        share(k, other)

    def passed_out(k, half):
        slab = index(x, half, core)
        for piece in halves:
            arrived(k, slab, piece)
            for who in (to_left, to_right):
                send(k, slab, piece, who)
        share(k, slab)

    def sides(k, half, onward):
        from_left, from_right = index(left, half, core), index(right_x, half, core)
        arrived(k, from_left, 0)
        if onward:
            send(k, from_left, 0, to_right)
        arrived(k, from_left, 1)
        arrived(k, from_right, 0)
        arrived(k, from_right, 1)
        if onward:
            send(k, from_right, 1, to_left)
        share(k, from_left)
        share(k, from_right)

    def far(k, half, onward):
        slab = index(across, half, core)
        for piece in halves:
            arrived(k, slab, piece)
            if onward:
                send(k + 2, slab, piece, to_next, unit=k)
        share(k, slab)

    def complete(k):
        group(k, 8, pass_sem.at[k], sibling_sem.at[k]).wait_recv()

    def first(k):
        for u in range(8):
            forward_block(u, t, s.at[k], right, forward, wide)

    def second(k):
        for i in range(4):
            middle_block(i // 2, i % 2, wide, middle, inverse, back)

    def third(k, emit=None):
        for u in range(8):
            backward_block(u, s.at[k], back, right, backward, acc, k == 0, emit)

    def emit(v, value):
        for i, tile in enumerate(swapped(value)):
            tiles[2 * v + i] = tile
            where = out_hbm.at[0, :, pl.ds(128 * (2 * v + i), 128)]
            pltpu.make_async_copy(tiles.at[2 * v + i], where, out_sem).start()

    pl.semaphore_wait(barrier, 6)
    for k in range(2):
        for piece in halves:
            send(k, mine, piece, to_z, source_hbm.at[k])
        for piece in halves:
            for who in (to_left, to_right):
                send(k, mine, piece, who, source_hbm.at[k])
        for piece in halves:
            send(k + 2, mine, piece, to_next, source_hbm.at[k], unit=k)
    for k in range(2):
        share(k, mine, source_hbm.at[k])
    pltpu.make_async_copy(tiles, tiles, target_sem).wait()
    swap_in(tiles, t)
    for copy in (*loads, *own):
        copy.wait()
    fill_inverse(lanes, rows, inverse)
    sides(0, hi, True)
    passed_out(2, near)
    sides(1, hi, True)
    passed_out(3, near)
    far(0, hi, True)
    other_out(0)
    sides(2, near, False)
    far(1, hi, True)
    sides(3, near, False)
    other_out(1)
    sides(0, 1 - hi, True)
    passed_out(2, 1 - near)
    far(0, 1 - hi, True)
    complete(0)
    first(0)
    sides(1, 1 - hi, True)
    passed_out(3, 1 - near)
    second(0)
    far(1, 1 - hi, True)
    sides(2, 1 - near, False)
    third(0)
    far(2, near, False)
    far(2, 1 - near, False)
    complete(1)
    first(1)
    sides(3, 1 - near, False)
    far(3, near, False)
    second(1)
    third(1)
    far(3, 1 - near, False)
    complete(2)
    first(2)
    second(2)
    third(2)
    complete(3)
    first(3)
    for k in range(UNITS):
        group(k, 8, pass_sem.at[k], sibling_sem.at[k]).wait_send()
        group(k, 11 if k < 2 else 4, link_sem.at[k], sibling_sem.at[k]).wait_send()
    second(3)
    third(3, emit)
    pltpu.make_async_copy(tiles, tiles, out_sem).wait()


def body(targets, sources):
    constants = [jnp.asarray(a) for a in tables()]
    slabs = sources.reshape(2, 4, 32, 128).transpose(0, 2, 1, 3).reshape(2, 16, 8, 128)
    anywhere = pl.BlockSpec(memory_space=pl.ANY)
    vmem, dma = pltpu.VMEM, pltpu.SemaphoreType.DMA
    return pl.pallas_call(
        kernel,
        out_shape=jax.ShapeDtypeStruct((1, 64, 4096), f32),
        in_specs=[anywhere] * 8,
        out_specs=anywhere,
        scratch_shapes=[
            vmem((32, 64, 128), f32), vmem((16, 16, 8, 128), f32), vmem((16, 16, 8, 128), f32),
            vmem((UNITS, 16, 16, 8, 128), f32),
            vmem((2, 2, 512, 256), bf16), vmem((2, 2, 256, 256), f32), vmem((2, 2, 256, 256), f32),
            *[vmem(a.shape, a.dtype) for a in constants],
            dma((UNITS,)), dma((UNITS,)), dma((UNITS, 16, 2)), dma((UNITS,)),
            dma((2,)), dma((6,)), dma, dma,
        ],
        compiler_params=pltpu.CompilerParams(
            collective_id=0, has_side_effects=True, vmem_limit_bytes=56 * 2**20
        ),
        name="exchange",
    )(targets, slabs, *constants)


def solution(mesh):
    return jax.shard_map(
        body,
        mesh=mesh,
        in_specs=(P(("band", "member"), None, None), P("band", "member", None)),
        out_specs=P(("band", "member"), None, None),
        check_vma=False,
    )
```

```python
import numpy as np
import jax
import jax.numpy as jnp
from jax import lax
from jax.experimental import pallas as pl
from jax.experimental.pallas import tpu as pltpu
from jax.sharding import PartitionSpec as P

bf16 = jnp.bfloat16
f32 = jnp.float32
MESH = pl.DeviceIdType.MESH
ROWS = 8
UNITS = 4


def split_table(table):
    high = np.asarray(table, np.float32).astype(bf16)
    low = (table - high.astype(np.float64)).astype(np.float32).astype(bf16)
    return high, low


def tables():
    wave = np.arange(64) + 1.0
    sine = np.sin(np.pi * np.outer(wave, wave) / 65)
    single = 4 * np.sin(np.pi * wave / 130) ** 2
    high, low = split_table(np.kron(np.eye(2), sine))
    right = np.block([[high, low], [high, low]])
    plane = np.broadcast_to(np.arange(64).reshape(16, 1, 4), (16, 2, 4)).reshape(-1)
    block = np.broadcast_to(np.arange(2).reshape(1, 2, 1), (16, 2, 4)).reshape(-1)
    out_wave, out_block = np.tile(np.arange(64), 2), np.repeat(np.arange(2), 64)
    left = sine[out_wave][:, plane] * (out_block[:, None] == block[None, :])
    high, low = split_table(left)
    forward = np.block([[high, high], [low, low]])
    high, low = split_table(left.T)
    backward = np.block([[high, high], [low, low]])
    middle = []
    for parity in range(2):
        one = np.kron(sine[parity::2, :32], np.eye(8))
        for matrix in (one, one.T):
            high, low = split_table(matrix)
            middle.append(np.concatenate([high, low], axis=1))
    middle = np.stack(middle).reshape(2, 2, 256, 512)
    pair, low3, bit, top, k3 = np.meshgrid(*[np.arange(n) for n in (2, 8, 2, 2, 64)], indexing="ij")
    lanes = single[32 * top + 8 * (2 * pair + bit) + low3] + single[k3]
    lanes = lanes.reshape(2, 8, 256).astype(np.float32)
    rows = np.repeat(single[:, None], 256, axis=1).astype(np.float32)
    return right, forward, backward, middle, lanes, rows


def split(x):
    high = x.astype(bf16)
    return high, (x - high.astype(f32)).astype(bf16)


def dot(a, b):
    return jnp.dot(a, b, preferred_element_type=f32)


def exchange(a, b, low):
    return jnp.where(low, a, pltpu.roll(b, 64, 1)), jnp.where(low, pltpu.roll(a, 64, 1), b)


def forward_block(u, t, s, right, forward, wide):
    low = lax.broadcasted_iota(jnp.int32, (32, 128), 1) < 64
    d = jnp.concatenate([(t[:, v] * s[:, v]).reshape(128, 128) for v in (u, 15 - u)], axis=0)
    dh, dl = split(d)
    y = dot(jnp.concatenate([dh, dl], axis=1), right[...])
    y = y[:, :128] + y[:, 128:]
    w = [jnp.concatenate([q[:128], q[128:]], axis=1) for q in split(y)]
    z = dot(forward[...], jnp.concatenate(w, axis=0))
    z = z[:128] + z[128:]
    x = {}
    for side in range(2):
        lanes = slice(128 * side, 128 * side + 128)
        for l in range(2):
            a, b = z[64 * l : 64 * l + 32, lanes], z[64 * l + 32 : 64 * l + 64, lanes]
            x[side, l, 0], x[side, l, 1] = exchange(a, b, low)
    pairs = [(x[0, l, i], x[1, 1 - l, 1 - i]) for l in range(2) for i in range(2)]
    start = pl.multiple_of(u * 32, 32)
    for parity, parts in ((0, [a + b for a, b in pairs]), (1, [a - b for a, b in pairs])):
        for g in range(4):
            lanes = slice(128 * (g % 2), 128 * (g % 2) + 128)
            high, rest = split(jnp.concatenate([q[8 * g : 8 * g + 8] for q in parts], axis=0))
            wide[parity, g // 2, pl.ds(start, 32), lanes] = high
            wide[parity, g // 2, pl.ds(256 + start, 32), lanes] = rest


def middle_block(parity, pair, wide, middle, inverse, back):
    def times(way, high, low):
        w = middle[parity, way]
        sides = jnp.concatenate([w[:, :256], w], axis=1)
        return dot(sides, jnp.concatenate([high, low, high], axis=0))

    e = wide[parity, pair]
    q = times(0, e[:256], e[256:]) * inverse[parity, pair]
    back[parity, pair] = times(1, *split(q))


def backward_block(u, s, back, right, backward, out, first, emit=None):
    low = lax.broadcasted_iota(jnp.int32, (32, 128), 1) < 64
    start = pl.multiple_of(u * 32, 32)
    total, differ = [[] for _ in range(4)], [[] for _ in range(4)]
    for g in range(4):
        lanes = slice(128 * (g % 2), 128 * (g % 2) + 128)
        even, odd = (back[p, g // 2, pl.ds(start, 32), lanes] for p in range(2))
        plus, minus = even + odd, even - odd
        for a in range(4):
            total[a].append(plus[8 * a : 8 * a + 8])
            differ[a].append(minus[8 * a : 8 * a + 8])
    total = [jnp.concatenate(q, axis=0) for q in total]
    differ = [jnp.concatenate(q, axis=0) for q in differ][::-1]
    z = []
    for side in (total, differ):
        z.append(jnp.concatenate([*exchange(side[0], side[1], low), *exchange(side[2], side[3], low)], axis=0))
    y = dot(backward[...], jnp.concatenate(split(jnp.concatenate(z, axis=1)), axis=0))
    y = y[:128] + y[128:]
    y = jnp.concatenate([y[:, :128], y[:, 128:]], axis=0)
    q = dot(jnp.concatenate(split(y), axis=1), right[...])
    q = q[:, :128] + q[:, 128:]
    for side, v in ((0, u), (1, 15 - u)):
        term = s[:, v] * q[128 * side : 128 * side + 128].reshape(16, 8, 128)
        if emit is None:
            out[:, v] = -term if first else out[:, v] - term
        else:
            emit(v, out[:, v] - term)


def swap_in(src, dst):
    top = lax.broadcasted_iota(jnp.int32, (8, 128), 0) < 4

    def step(v, carry):
        for i in range(8):
            a, b = src[2 * v, 8 * i : 8 * i + 8], src[2 * v + 1, 8 * i : 8 * i + 8]
            dst[2 * i, v] = jnp.where(top, a, pltpu.roll(b, 4, 0))
            dst[2 * i + 1, v] = jnp.where(top, pltpu.roll(a, 4, 0), b)
        return carry

    lax.fori_loop(0, 16, step, 0)


def swapped(value):
    top = lax.broadcasted_iota(jnp.int32, (8, 8, 128), 1) < 4
    value = value.reshape(8, 2, 8, 128)
    a, b = value[:, 0], value[:, 1]
    one, two = jnp.where(top, a, pltpu.roll(b, 4, 1)), jnp.where(top, pltpu.roll(a, 4, 1), b)
    return one.reshape(64, 128), two.reshape(64, 128)


def fill_inverse(lanes, rows, inverse):
    factor = (2.0 / 65) ** 3

    def step(m, carry):
        start = pl.multiple_of(8 * m, 8)
        for parity in range(2):
            for pair in range(2):
                eigen = lanes[pair] + rows[pl.ds(2 * m + parity, 1), :]
                inverse[parity, pair, pl.ds(start, 8), :] = factor / eigen
        return carry

    lax.fori_loop(0, 32, step, 0)


def kernel(
    target_hbm, source_hbm, right_hbm, forward_hbm, backward_hbm, middle_hbm, lanes_hbm, rows_hbm,
    out_hbm,
    tiles, t, acc, s, wide, back, inverse, right, forward, backward, middle, lanes, rows,
    link_sem, pass_sem, recv_sem, sibling_sem, own_sem, table_sem, target_sem, out_sem,
):
    band, m = lax.axis_index("band"), lax.axis_index("member")
    bands = lax.axis_size("band")
    columns = bands // 4
    column = band % columns
    x, hi, core = m // 4, (m // 2) % 2, m % 2
    index = lambda x, hi, core: x * 4 + hi * 2 + core
    left, right_x, across = (x + 3) % 4, (x + 1) % 4, (x + 2) % 4
    to_wrap = jnp.where(column == columns - 1, 1, 0)
    from_wrap = jnp.where(column == 0, 1, 0)
    to_sibling = {"member": index(x, hi, 1 - core)}
    to_z = {"member": index(x, 1 - hi, core)}
    to_left, to_right = ({"member": index(xx, hi, core)} for xx in (left, right_x))
    to_next = {"band": (band + 1) % bands}
    to_prev = {"band": (band + bands - 1) % bands}

    barrier = pltpu.get_barrier_semaphore()
    for who in (to_z, to_left, to_right, to_next, to_prev, to_sibling):
        pl.semaphore_signal(barrier, inc=1, device_id=who, device_id_type=MESH)

    loads = [
        pltpu.make_async_copy(a, b, table_sem.at[i])
        for i, (a, b) in enumerate(
            ((right_hbm, right), (forward_hbm, forward), (backward_hbm, backward),
             (middle_hbm, middle), (lanes_hbm, lanes), (rows_hbm, rows))
        )
    ]
    own = [pltpu.make_async_copy(source_hbm.at[k], s.at[k, m], own_sem.at[k]) for k in range(2)]
    for copy in (*own, *loads):
        copy.start()
    for i in range(32):
        pltpu.make_async_copy(target_hbm.at[0, :, pl.ds(128 * i, 128)], tiles.at[i], target_sem).start()

    def remote(k, slab, piece, who, src, unit):
        window = pl.ds(ROWS * piece, ROWS)
        return pltpu.make_async_remote_copy(
            src_ref=s.at[unit, slab, window] if src is None else src.at[window],
            dst_ref=s.at[k, slab, window],
            send_sem=link_sem.at[unit],
            recv_sem=recv_sem.at[k, slab, piece],
            device_id=who,
            device_id_type=MESH,
        )

    def send(k, slab, piece, who, src=None, unit=None):
        remote(k, slab, piece, who, src, k if unit is None else unit).start()

    def arrived(k, slab, piece):
        remote(k, slab, piece, to_left, None, k).wait_recv()

    def share(k, slab, src=None):
        pltpu.make_async_remote_copy(
            src_ref=s.at[k, slab] if src is None else src,
            dst_ref=s.at[k, slab],
            send_sem=pass_sem.at[k],
            recv_sem=sibling_sem.at[k],
            device_id=to_sibling,
            device_id_type=MESH,
        ).start()

    def group(k, count, send_sem, recv_sem):
        block = s.at[k, pl.ds(0, count)]
        return pltpu.make_async_remote_copy(
            src_ref=block, dst_ref=block, send_sem=send_sem, recv_sem=recv_sem,
            device_id=to_sibling, device_id_type=MESH,
        )

    mine, other = index(x, hi, core), index(x, 1 - hi, core)
    pieces = range(16 // ROWS)

    def own_next():
        for k in range(2):
            for piece in pieces:
                send(k + 2, mine, piece, to_next, source_hbm.at[k], unit=k)

    def passed(wrap, *which):
        @pl.when(from_wrap == wrap)
        def _():
            for k, half in which:
                passed_out(k, half)

    def other_out(k, some=pieces):
        for piece in some:
            arrived(k, other, piece)
            for who in (to_left, to_right):
                send(k, other, piece, who)
            send(k + 2, other, piece, to_next, unit=k)
        if pieces[-1] in some:
            share(k, other)

    def passed_out(k, half):
        slab = index(x, half, core)
        for piece in pieces:
            arrived(k, slab, piece)
            for who in (to_left, to_right):
                send(k, slab, piece, who)
        share(k, slab)

    def sides(k, half):
        from_left, from_right = index(left, half, core), index(right_x, half, core)

        def relay(piece):
            if piece < len(pieces) // 2:
                send(k, from_left, piece, to_right)
            else:
                send(k, from_right, piece, to_left)

        for piece in pieces:
            arrived(k, from_left, piece)
            arrived(k, from_right, piece)
            if k < 2:
                relay(piece)
        if k >= 2:
            @pl.when(from_wrap == 1)
            def _():
                for piece in pieces:
                    relay(piece)

        share(k, from_left)
        share(k, from_right)

    def far(k, half):
        slab = index(across, half, core)
        for piece in pieces:
            arrived(k, slab, piece)
        if k < 2:
            @pl.when(to_wrap == 0)
            def _():
                for piece in pieces:
                    send(k + 2, slab, piece, to_next, unit=k)

        share(k, slab)

    def sent(k):
        group(k, 8, pass_sem.at[k], sibling_sem.at[k]).wait_send()
        flag = to_wrap if k < 2 else from_wrap
        for value, count in ((0, 11 if k < 2 else 4), (1, 9 if k < 2 else 6)):
            @pl.when(flag == value)
            def _():
                group(k, count, link_sem.at[k], sibling_sem.at[k]).wait_send()

    def complete(k):
        group(k, 8, pass_sem.at[k], sibling_sem.at[k]).wait_recv()

    def first(k):
        for u in range(8):
            forward_block(u, t, s.at[k], right, forward, wide)

    def second(k):
        for i in range(4):
            middle_block(i // 2, i % 2, wide, middle, inverse, back)

    def third(k, emit=None):
        for u in range(8):
            backward_block(u, s.at[k], back, right, backward, acc, k == 0, emit)

    def emit(v, value):
        for i, tile in enumerate(swapped(value)):
            tiles[2 * v + i] = tile
            where = out_hbm.at[0, :, pl.ds(128 * (2 * v + i), 128)]
            pltpu.make_async_copy(tiles.at[2 * v + i], where, out_sem).start()

    pl.semaphore_wait(barrier, 6)
    for k in range(2):
        for piece in pieces:
            send(k, mine, piece, to_z, source_hbm.at[k])
        for piece in pieces:
            for who in (to_left, to_right):
                send(k, mine, piece, who, source_hbm.at[k])
        if k == 0:
            pl.when(to_wrap == 0)(own_next)
    for k in range(2):
        share(k, mine, source_hbm.at[k])
    pltpu.make_async_copy(tiles, tiles, target_sem).wait()
    swap_in(tiles, t)
    for copy in (*loads, *own):
        copy.wait()
    fill_inverse(lanes, rows, inverse)
    sides(0, hi)
    sides(1, hi)
    passed(0, (2, hi))
    pl.when(to_wrap == 1)(own_next)
    other_out(0)
    far(0, hi)
    passed(0, (3, hi))
    other_out(1)
    sides(0, 1 - hi)
    passed(1, (2, hi))
    far(1, hi)
    passed(0, (2, 1 - hi))
    far(0, 1 - hi)
    passed(1, (3, hi))
    sides(1, 1 - hi)
    complete(0)
    first(0)
    passed(0, (3, 1 - hi))
    passed(1, (2, 1 - hi), (3, 1 - hi))
    sides(2, hi)
    second(0)
    far(1, 1 - hi)
    sides(3, hi)
    third(0)
    sides(2, 1 - hi)
    complete(1)
    first(1)
    far(2, hi)
    sides(3, 1 - hi)
    second(1)
    far(2, 1 - hi)
    third(1)
    far(3, hi)
    far(3, 1 - hi)
    complete(2)
    first(2)
    second(2)
    third(2)
    complete(3)
    first(3)
    for k in range(UNITS):
        sent(k)
    second(3)
    third(3, emit)
    pltpu.make_async_copy(tiles, tiles, out_sem).wait()


def body(targets, sources):
    constants = [jnp.asarray(a) for a in tables()]
    slabs = sources.reshape(2, 4, 32, 128).transpose(0, 2, 1, 3).reshape(2, 16, 8, 128)
    anywhere = pl.BlockSpec(memory_space=pl.ANY)
    vmem, dma = pltpu.VMEM, pltpu.SemaphoreType.DMA
    return pl.pallas_call(
        kernel,
        out_shape=jax.ShapeDtypeStruct((1, 64, 4096), f32),
        in_specs=[anywhere] * 8,
        out_specs=anywhere,
        scratch_shapes=[
            vmem((32, 64, 128), f32), vmem((16, 16, 8, 128), f32), vmem((16, 16, 8, 128), f32),
            vmem((UNITS, 16, 16, 8, 128), f32),
            vmem((2, 2, 512, 256), bf16), vmem((2, 2, 256, 256), f32), vmem((2, 2, 256, 256), f32),
            *[vmem(a.shape, a.dtype) for a in constants],
            dma((UNITS,)), dma((UNITS,)), dma((UNITS, 16, 16 // ROWS)), dma((UNITS,)),
            dma((2,)), dma((6,)), dma, dma,
        ],
        compiler_params=pltpu.CompilerParams(
            collective_id=0, has_side_effects=True, vmem_limit_bytes=56 * 2**20
        ),
        name="exchange",
    )(targets, slabs, *constants)


def solution(mesh):
    return jax.shard_map(
        body,
        mesh=mesh,
        in_specs=(P(("band", "member"), None, None), P("band", "member", None)),
        out_specs=P(("band", "member"), None, None),
        check_vma=False,
    )
```

```python
import numpy as np
import jax
import jax.numpy as jnp
from jax import lax
from jax.experimental import pallas as pl
from jax.experimental.pallas import tpu as pltpu
from jax.sharding import PartitionSpec as P

bf16 = jnp.bfloat16
f32 = jnp.float32
MESH = pl.DeviceIdType.MESH
ROWS = 8
UNITS = 4


def split_table(table):
    high = np.asarray(table, np.float32).astype(bf16)
    low = (table - high.astype(np.float64)).astype(np.float32).astype(bf16)
    return high, low


def tables():
    wave = np.arange(64) + 1.0
    sine = np.sin(np.pi * np.outer(wave, wave) / 65)
    single = 4 * np.sin(np.pi * wave / 130) ** 2
    high, low = split_table(np.kron(np.eye(2), sine))
    right = np.block([[high, low], [high, low]])
    plane = np.broadcast_to(np.arange(64).reshape(16, 1, 4), (16, 2, 4)).reshape(-1)
    block = np.broadcast_to(np.arange(2).reshape(1, 2, 1), (16, 2, 4)).reshape(-1)
    out_wave, out_block = np.tile(np.arange(64), 2), np.repeat(np.arange(2), 64)
    left = sine[out_wave][:, plane] * (out_block[:, None] == block[None, :])
    high, low = split_table(left)
    forward = np.block([[high, high], [low, low]])
    high, low = split_table(left.T)
    backward = np.block([[high, high], [low, low]])
    middle = []
    for parity in range(2):
        one = np.kron(sine[parity::2, :32], np.eye(8))
        for matrix in (one, one.T):
            high, low = split_table(matrix)
            middle.append(np.concatenate([high, low], axis=1))
    middle = np.stack(middle).reshape(2, 2, 256, 512)
    pair, low3, bit, top, k3 = np.meshgrid(*[np.arange(n) for n in (2, 8, 2, 2, 64)], indexing="ij")
    lanes = single[32 * top + 8 * (2 * pair + bit) + low3] + single[k3]
    lanes = lanes.reshape(2, 8, 256).astype(np.float32)
    rows = np.repeat(single[:, None], 256, axis=1).astype(np.float32)
    return right, forward, backward, middle, lanes, rows


def split(x):
    high = x.astype(bf16)
    return high, (x - high.astype(f32)).astype(bf16)


def dot(a, b):
    return jnp.dot(a, b, preferred_element_type=f32)


def exchange(a, b, low):
    return jnp.where(low, a, pltpu.roll(b, 64, 1)), jnp.where(low, pltpu.roll(a, 64, 1), b)


def forward_block(u, t, s, right, forward, wide):
    low = lax.broadcasted_iota(jnp.int32, (32, 128), 1) < 64
    d = jnp.concatenate([(t[:, v] * s[:, v]).reshape(128, 128) for v in (u, 15 - u)], axis=0)
    dh, dl = split(d)
    y = dot(jnp.concatenate([dh, dl], axis=1), right[...])
    y = y[:, :128] + y[:, 128:]
    w = [jnp.concatenate([q[:128], q[128:]], axis=1) for q in split(y)]
    z = dot(forward[...], jnp.concatenate(w, axis=0))
    z = z[:128] + z[128:]
    x = {}
    for side in range(2):
        lanes = slice(128 * side, 128 * side + 128)
        for l in range(2):
            a, b = z[64 * l : 64 * l + 32, lanes], z[64 * l + 32 : 64 * l + 64, lanes]
            x[side, l, 0], x[side, l, 1] = exchange(a, b, low)
    pairs = [(x[0, l, i], x[1, 1 - l, 1 - i]) for l in range(2) for i in range(2)]
    start = pl.multiple_of(u * 32, 32)
    for parity, parts in ((0, [a + b for a, b in pairs]), (1, [a - b for a, b in pairs])):
        for g in range(4):
            lanes = slice(128 * (g % 2), 128 * (g % 2) + 128)
            high, rest = split(jnp.concatenate([q[8 * g : 8 * g + 8] for q in parts], axis=0))
            wide[parity, g // 2, pl.ds(start, 32), lanes] = high
            wide[parity, g // 2, pl.ds(256 + start, 32), lanes] = rest


def middle_block(parity, pair, wide, middle, inverse, back):
    def times(way, high, low):
        w = middle[parity, way]
        sides = jnp.concatenate([w[:, :256], w], axis=1)
        return dot(sides, jnp.concatenate([high, low, high], axis=0))

    e = wide[parity, pair]
    q = times(0, e[:256], e[256:]) * inverse[parity, pair]
    back[parity, pair] = times(1, *split(q))


def backward_block(u, s, back, right, backward, out, first, emit=None):
    low = lax.broadcasted_iota(jnp.int32, (32, 128), 1) < 64
    start = pl.multiple_of(u * 32, 32)
    total, differ = [[] for _ in range(4)], [[] for _ in range(4)]
    for g in range(4):
        lanes = slice(128 * (g % 2), 128 * (g % 2) + 128)
        even, odd = (back[p, g // 2, pl.ds(start, 32), lanes] for p in range(2))
        plus, minus = even + odd, even - odd
        for a in range(4):
            total[a].append(plus[8 * a : 8 * a + 8])
            differ[a].append(minus[8 * a : 8 * a + 8])
    total = [jnp.concatenate(q, axis=0) for q in total]
    differ = [jnp.concatenate(q, axis=0) for q in differ][::-1]
    z = []
    for side in (total, differ):
        z.append(jnp.concatenate([*exchange(side[0], side[1], low), *exchange(side[2], side[3], low)], axis=0))
    y = dot(backward[...], jnp.concatenate(split(jnp.concatenate(z, axis=1)), axis=0))
    y = y[:128] + y[128:]
    y = jnp.concatenate([y[:, :128], y[:, 128:]], axis=0)
    q = dot(jnp.concatenate(split(y), axis=1), right[...])
    q = q[:, :128] + q[:, 128:]
    for side, v in ((0, u), (1, 15 - u)):
        term = s[:, v] * q[128 * side : 128 * side + 128].reshape(16, 8, 128)
        if emit is None:
            out[:, v] = -term if first else out[:, v] - term
        else:
            emit(v, out[:, v] - term)


def swap_in(src, dst):
    top = lax.broadcasted_iota(jnp.int32, (8, 128), 0) < 4

    def step(v, carry):
        for i in range(8):
            a, b = src[2 * v, 8 * i : 8 * i + 8], src[2 * v + 1, 8 * i : 8 * i + 8]
            dst[2 * i, v] = jnp.where(top, a, pltpu.roll(b, 4, 0))
            dst[2 * i + 1, v] = jnp.where(top, pltpu.roll(a, 4, 0), b)
        return carry

    lax.fori_loop(0, 16, step, 0)


def swapped(value):
    top = lax.broadcasted_iota(jnp.int32, (8, 8, 128), 1) < 4
    value = value.reshape(8, 2, 8, 128)
    a, b = value[:, 0], value[:, 1]
    one, two = jnp.where(top, a, pltpu.roll(b, 4, 1)), jnp.where(top, pltpu.roll(a, 4, 1), b)
    return one.reshape(64, 128), two.reshape(64, 128)


def fill_inverse(lanes, rows, inverse):
    factor = (2.0 / 65) ** 3

    def step(m, carry):
        start = pl.multiple_of(8 * m, 8)
        for parity in range(2):
            for pair in range(2):
                eigen = lanes[pair] + rows[pl.ds(2 * m + parity, 1), :]
                inverse[parity, pair, pl.ds(start, 8), :] = factor / eigen
        return carry

    lax.fori_loop(0, 32, step, 0)


def kernel(
    target_hbm, source_hbm, right_hbm, forward_hbm, backward_hbm, middle_hbm, lanes_hbm, rows_hbm,
    out_hbm,
    tiles, t, acc, s, wide, back, inverse, right, forward, backward, middle, lanes, rows,
    link_sem, pass_sem, recv_sem, sibling_sem, own_sem, table_sem, target_sem, out_sem,
):
    band, m = lax.axis_index("band"), lax.axis_index("member")
    bands = lax.axis_size("band")
    columns = bands // 4
    column = band % columns
    x, hi, core = m // 4, (m // 2) % 2, m % 2
    index = lambda x, hi, core: x * 4 + hi * 2 + core
    left, right_x, across = (x + 3) % 4, (x + 1) % 4, (x + 2) % 4
    to_wrap = jnp.where(column == columns - 1, 1, 0)
    from_wrap = jnp.where(column == 0, 1, 0)
    to_sibling = {"member": index(x, hi, 1 - core)}
    to_z = {"member": index(x, 1 - hi, core)}
    to_left, to_right = ({"member": index(xx, hi, core)} for xx in (left, right_x))
    to_next = {"band": (band + 1) % bands}
    to_prev = {"band": (band + bands - 1) % bands}

    barrier = pltpu.get_barrier_semaphore()
    for who in (to_z, to_left, to_right, to_next, to_prev, to_sibling):
        pl.semaphore_signal(barrier, inc=1, device_id=who, device_id_type=MESH)

    loads = [
        pltpu.make_async_copy(a, b, table_sem.at[i])
        for i, (a, b) in enumerate(
            ((right_hbm, right), (forward_hbm, forward), (backward_hbm, backward),
             (middle_hbm, middle), (lanes_hbm, lanes), (rows_hbm, rows))
        )
    ]
    own = [pltpu.make_async_copy(source_hbm.at[k], s.at[k, m], own_sem.at[k]) for k in range(2)]
    for copy in (*own, *loads):
        copy.start()
    for i in range(32):
        pltpu.make_async_copy(target_hbm.at[0, :, pl.ds(128 * i, 128)], tiles.at[i], target_sem).start()

    def remote(k, slab, piece, who, src, unit):
        window = pl.ds(ROWS * piece, ROWS)
        return pltpu.make_async_remote_copy(
            src_ref=s.at[unit, slab, window] if src is None else src.at[window],
            dst_ref=s.at[k, slab, window],
            send_sem=link_sem.at[unit],
            recv_sem=recv_sem.at[k, slab, piece],
            device_id=who,
            device_id_type=MESH,
        )

    def send(k, slab, piece, who, src=None, unit=None):
        remote(k, slab, piece, who, src, k if unit is None else unit).start()

    def arrived(k, slab, piece):
        remote(k, slab, piece, to_left, None, k).wait_recv()

    def share(k, slab, src=None):
        pltpu.make_async_remote_copy(
            src_ref=s.at[k, slab] if src is None else src,
            dst_ref=s.at[k, slab],
            send_sem=pass_sem.at[k],
            recv_sem=sibling_sem.at[k],
            device_id=to_sibling,
            device_id_type=MESH,
        ).start()

    def group(k, count, send_sem, recv_sem):
        block = s.at[k, pl.ds(0, count)]
        return pltpu.make_async_remote_copy(
            src_ref=block, dst_ref=block, send_sem=send_sem, recv_sem=recv_sem,
            device_id=to_sibling, device_id_type=MESH,
        )

    mine, other = index(x, hi, core), index(x, 1 - hi, core)
    pieces = range(16 // ROWS)

    def other_out(k, some=pieces):
        for piece in some:
            arrived(k, other, piece)
            for who in (to_left, to_right):
                send(k, other, piece, who)
            send(k + 2, other, piece, to_next, unit=k)
        if pieces[-1] in some:
            share(k, other)

    def passed_out(k, half):
        slab = index(x, half, core)
        for piece in pieces:
            arrived(k, slab, piece)
            for who in (to_left, to_right):
                send(k, slab, piece, who)
        share(k, slab)

    def sides(k, half):
        from_left, from_right = index(left, half, core), index(right_x, half, core)

        def relay(piece):
            if piece < len(pieces) // 2:
                send(k, from_left, piece, to_right)
            else:
                send(k, from_right, piece, to_left)

        for piece in pieces:
            arrived(k, from_left, piece)
            arrived(k, from_right, piece)
            if k < 2:
                relay(piece)
        if k >= 2:
            @pl.when(from_wrap == 1)
            def _():
                for piece in pieces:
                    relay(piece)

        share(k, from_left)
        share(k, from_right)

    def far(k, half):
        slab = index(across, half, core)
        for piece in pieces:
            arrived(k, slab, piece)
        if k < 2:
            @pl.when(to_wrap == 0)
            def _():
                for piece in pieces:
                    send(k + 2, slab, piece, to_next, unit=k)

        share(k, slab)

    def sent(k):
        group(k, 8, pass_sem.at[k], sibling_sem.at[k]).wait_send()
        flag = to_wrap if k < 2 else from_wrap
        for value, count in ((0, 11 if k < 2 else 4), (1, 9 if k < 2 else 6)):
            @pl.when(flag == value)
            def _():
                group(k, count, link_sem.at[k], sibling_sem.at[k]).wait_send()

    def complete(k):
        group(k, 8, pass_sem.at[k], sibling_sem.at[k]).wait_recv()

    def first(k):
        for u in range(8):
            forward_block(u, t, s.at[k], right, forward, wide)

    def second(k):
        for i in range(4):
            middle_block(i // 2, i % 2, wide, middle, inverse, back)

    def third(k, emit=None):
        for u in range(8):
            backward_block(u, s.at[k], back, right, backward, acc, k == 0, emit)

    def emit(v, value):
        for i, tile in enumerate(swapped(value)):
            tiles[2 * v + i] = tile
            where = out_hbm.at[0, :, pl.ds(128 * (2 * v + i), 128)]
            pltpu.make_async_copy(tiles.at[2 * v + i], where, out_sem).start()

    pl.semaphore_wait(barrier, 6)
    for k in range(2):
        for piece in pieces:
            send(k, mine, piece, to_z, source_hbm.at[k])
        for piece in pieces:
            for who in (to_left, to_right):
                send(k, mine, piece, who, source_hbm.at[k])
        for piece in pieces:
            send(k + 2, mine, piece, to_next, source_hbm.at[k], unit=k)
    for k in range(2):
        share(k, mine, source_hbm.at[k])
    pltpu.make_async_copy(tiles, tiles, target_sem).wait()
    swap_in(tiles, t)
    for copy in (*loads, *own):
        copy.wait()
    fill_inverse(lanes, rows, inverse)
    sides(0, hi)
    sides(1, hi)
    passed_out(2, hi)
    other_out(0)
    far(0, hi)
    passed_out(3, hi)
    sides(0, 1 - hi)
    far(1, hi)
    sides(2, hi)
    other_out(1)
    sides(3, hi)
    far(0, 1 - hi)
    passed_out(2, 1 - hi)
    complete(0)
    first(0)
    sides(1, 1 - hi)
    passed_out(3, 1 - hi)
    sides(2, 1 - hi)
    second(0)
    far(1, 1 - hi)
    third(0)
    far(2, hi)
    sides(3, 1 - hi)
    complete(1)
    first(1)
    far(2, 1 - hi)
    far(3, hi)
    second(1)
    far(3, 1 - hi)
    third(1)
    complete(2)
    first(2)
    second(2)
    third(2)
    complete(3)
    first(3)
    for k in range(UNITS):
        sent(k)
    second(3)
    third(3, emit)
    pltpu.make_async_copy(tiles, tiles, out_sem).wait()


def body(targets, sources):
    constants = [jnp.asarray(a) for a in tables()]
    slabs = sources.reshape(2, 4, 32, 128).transpose(0, 2, 1, 3).reshape(2, 16, 8, 128)
    anywhere = pl.BlockSpec(memory_space=pl.ANY)
    vmem, dma = pltpu.VMEM, pltpu.SemaphoreType.DMA
    return pl.pallas_call(
        kernel,
        out_shape=jax.ShapeDtypeStruct((1, 64, 4096), f32),
        in_specs=[anywhere] * 8,
        out_specs=anywhere,
        scratch_shapes=[
            vmem((32, 64, 128), f32), vmem((16, 16, 8, 128), f32), vmem((16, 16, 8, 128), f32),
            vmem((UNITS, 16, 16, 8, 128), f32),
            vmem((2, 2, 512, 256), bf16), vmem((2, 2, 256, 256), f32), vmem((2, 2, 256, 256), f32),
            *[vmem(a.shape, a.dtype) for a in constants],
            dma((UNITS,)), dma((UNITS,)), dma((UNITS, 16, 16 // ROWS)), dma((UNITS,)),
            dma((2,)), dma((6,)), dma, dma,
        ],
        compiler_params=pltpu.CompilerParams(
            collective_id=0, has_side_effects=True, vmem_limit_bytes=56 * 2**20
        ),
        name="exchange",
    )(targets, slabs, *constants)


def solution(mesh):
    return jax.shard_map(
        body,
        mesh=mesh,
        in_specs=(P(("band", "member"), None, None), P("band", "member", None)),
        out_specs=P(("band", "member"), None, None),
        check_vma=False,
    )
```

```python
import numpy as np
import jax
import jax.numpy as jnp
from jax import lax
from jax.experimental import pallas as pl
from jax.experimental.pallas import tpu as pltpu
from jax.sharding import PartitionSpec as P

bf16 = jnp.bfloat16
f32 = jnp.float32
MESH = pl.DeviceIdType.MESH
ROWS = 8
UNITS = 4


def split_table(table):
    high = np.asarray(table, np.float32).astype(bf16)
    low = (table - high.astype(np.float64)).astype(np.float32).astype(bf16)
    return high, low


def tables():
    wave = np.arange(64) + 1.0
    sine = np.sin(np.pi * np.outer(wave, wave) / 65)
    single = 4 * np.sin(np.pi * wave / 130) ** 2
    high, low = split_table(np.kron(np.eye(2), sine))
    right = np.block([[high, low], [high, low]])
    plane = np.broadcast_to(np.arange(64).reshape(16, 1, 4), (16, 2, 4)).reshape(-1)
    block = np.broadcast_to(np.arange(2).reshape(1, 2, 1), (16, 2, 4)).reshape(-1)
    out_wave, out_block = np.tile(np.arange(64), 2), np.repeat(np.arange(2), 64)
    left = sine[out_wave][:, plane] * (out_block[:, None] == block[None, :])
    high, low = split_table(left)
    forward = np.block([[high, high], [low, low]])
    high, low = split_table(left.T)
    backward = np.block([[high, high], [low, low]])
    middle = []
    for parity in range(2):
        one = np.kron(sine[parity::2, :32], np.eye(8))
        for matrix in (one, one.T):
            high, low = split_table(matrix)
            middle.append(np.concatenate([high, low], axis=1))
    middle = np.stack(middle).reshape(2, 2, 256, 512)
    pair, low3, bit, top, k3 = np.meshgrid(*[np.arange(n) for n in (2, 8, 2, 2, 64)], indexing="ij")
    lanes = single[32 * top + 8 * (2 * pair + bit) + low3] + single[k3]
    lanes = lanes.reshape(2, 8, 256).astype(np.float32)
    rows = np.repeat(single[:, None], 256, axis=1).astype(np.float32)
    return right, forward, backward, middle, lanes, rows


def split(x):
    high = x.astype(bf16)
    return high, (x - high.astype(f32)).astype(bf16)


def dot(a, b):
    return jnp.dot(a, b, preferred_element_type=f32)


def exchange(a, b, low):
    return jnp.where(low, a, pltpu.roll(b, 64, 1)), jnp.where(low, pltpu.roll(a, 64, 1), b)


def forward_block(u, t, s, right, forward, wide):
    low = lax.broadcasted_iota(jnp.int32, (32, 128), 1) < 64
    d = jnp.concatenate([(t[:, v] * s[:, v]).reshape(128, 128) for v in (u, 15 - u)], axis=0)
    dh, dl = split(d)
    y = dot(jnp.concatenate([dh, dl], axis=1), right[...])
    y = y[:, :128] + y[:, 128:]
    w = [jnp.concatenate([q[:128], q[128:]], axis=1) for q in split(y)]
    z = dot(forward[...], jnp.concatenate(w, axis=0))
    z = z[:128] + z[128:]
    x = {}
    for side in range(2):
        lanes = slice(128 * side, 128 * side + 128)
        for l in range(2):
            a, b = z[64 * l : 64 * l + 32, lanes], z[64 * l + 32 : 64 * l + 64, lanes]
            x[side, l, 0], x[side, l, 1] = exchange(a, b, low)
    pairs = [(x[0, l, i], x[1, 1 - l, 1 - i]) for l in range(2) for i in range(2)]
    start = pl.multiple_of(u * 32, 32)
    for parity, parts in ((0, [a + b for a, b in pairs]), (1, [a - b for a, b in pairs])):
        for g in range(4):
            lanes = slice(128 * (g % 2), 128 * (g % 2) + 128)
            high, rest = split(jnp.concatenate([q[8 * g : 8 * g + 8] for q in parts], axis=0))
            wide[parity, g // 2, pl.ds(start, 32), lanes] = high
            wide[parity, g // 2, pl.ds(256 + start, 32), lanes] = rest


def middle_block(parity, pair, wide, middle, inverse, back):
    def times(way, high, low):
        w = middle[parity, way]
        sides = jnp.concatenate([w[:, :256], w], axis=1)
        return dot(sides, jnp.concatenate([high, low, high], axis=0))

    e = wide[parity, pair]
    q = times(0, e[:256], e[256:]) * inverse[parity, pair]
    back[parity, pair] = times(1, *split(q))


def backward_block(u, s, back, right, backward, out, first, emit=None):
    low = lax.broadcasted_iota(jnp.int32, (32, 128), 1) < 64
    start = pl.multiple_of(u * 32, 32)
    total, differ = [[] for _ in range(4)], [[] for _ in range(4)]
    for g in range(4):
        lanes = slice(128 * (g % 2), 128 * (g % 2) + 128)
        even, odd = (back[p, g // 2, pl.ds(start, 32), lanes] for p in range(2))
        plus, minus = even + odd, even - odd
        for a in range(4):
            total[a].append(plus[8 * a : 8 * a + 8])
            differ[a].append(minus[8 * a : 8 * a + 8])
    total = [jnp.concatenate(q, axis=0) for q in total]
    differ = [jnp.concatenate(q, axis=0) for q in differ][::-1]
    z = []
    for side in (total, differ):
        z.append(jnp.concatenate([*exchange(side[0], side[1], low), *exchange(side[2], side[3], low)], axis=0))
    y = dot(backward[...], jnp.concatenate(split(jnp.concatenate(z, axis=1)), axis=0))
    y = y[:128] + y[128:]
    y = jnp.concatenate([y[:, :128], y[:, 128:]], axis=0)
    q = dot(jnp.concatenate(split(y), axis=1), right[...])
    q = q[:, :128] + q[:, 128:]
    for side, v in ((0, u), (1, 15 - u)):
        term = s[:, v] * q[128 * side : 128 * side + 128].reshape(16, 8, 128)
        if emit is None:
            out[:, v] = -term if first else out[:, v] - term
        else:
            emit(v, out[:, v] - term)


def swap_in(src, dst):
    top = lax.broadcasted_iota(jnp.int32, (8, 128), 0) < 4

    def step(v, carry):
        for i in range(8):
            a, b = src[2 * v, 8 * i : 8 * i + 8], src[2 * v + 1, 8 * i : 8 * i + 8]
            dst[2 * i, v] = jnp.where(top, a, pltpu.roll(b, 4, 0))
            dst[2 * i + 1, v] = jnp.where(top, pltpu.roll(a, 4, 0), b)
        return carry

    lax.fori_loop(0, 16, step, 0)


def swapped(value):
    top = lax.broadcasted_iota(jnp.int32, (8, 8, 128), 1) < 4
    value = value.reshape(8, 2, 8, 128)
    a, b = value[:, 0], value[:, 1]
    one, two = jnp.where(top, a, pltpu.roll(b, 4, 1)), jnp.where(top, pltpu.roll(a, 4, 1), b)
    return one.reshape(64, 128), two.reshape(64, 128)


def fill_inverse(lanes, rows, inverse):
    factor = (2.0 / 65) ** 3

    def step(m, carry):
        start = pl.multiple_of(8 * m, 8)
        for parity in range(2):
            for pair in range(2):
                eigen = lanes[pair] + rows[pl.ds(2 * m + parity, 1), :]
                inverse[parity, pair, pl.ds(start, 8), :] = factor / eigen
        return carry

    lax.fori_loop(0, 32, step, 0)


def kernel(
    target_hbm, source_hbm, right_hbm, forward_hbm, backward_hbm, middle_hbm, lanes_hbm, rows_hbm,
    out,
    tiles, t, acc, s, wide, back, inverse, right, forward, backward, middle, lanes, rows,
    link_sem, pass_sem, recv_sem, sibling_sem, own_sem, table_sem, target_sem,
):
    band, m = lax.axis_index("band"), lax.axis_index("member")
    bands = lax.axis_size("band")
    columns = bands // 4
    column = band % columns
    x, hi, core = m // 4, (m // 2) % 2, m % 2
    index = lambda x, hi, core: x * 4 + hi * 2 + core
    left, right_x, across = (x + 3) % 4, (x + 1) % 4, (x + 2) % 4
    to_wrap = jnp.where(column == columns - 1, 1, 0)
    from_wrap = jnp.where(column == 0, 1, 0)
    to_sibling = {"member": index(x, hi, 1 - core)}
    to_z = {"member": index(x, 1 - hi, core)}
    to_left, to_right = ({"member": index(xx, hi, core)} for xx in (left, right_x))
    to_next = {"band": (band + 1) % bands}
    to_prev = {"band": (band + bands - 1) % bands}

    barrier = pltpu.get_barrier_semaphore()
    for who in (to_z, to_left, to_right, to_next, to_prev, to_sibling):
        pl.semaphore_signal(barrier, inc=1, device_id=who, device_id_type=MESH)

    loads = [
        pltpu.make_async_copy(a, b, table_sem.at[i])
        for i, (a, b) in enumerate(
            ((right_hbm, right), (forward_hbm, forward), (backward_hbm, backward),
             (middle_hbm, middle), (lanes_hbm, lanes), (rows_hbm, rows))
        )
    ]
    own = [pltpu.make_async_copy(source_hbm.at[k], s.at[k, m], own_sem.at[k]) for k in range(2)]
    for copy in (*own, *loads):
        copy.start()
    for i in range(32):
        pltpu.make_async_copy(target_hbm.at[0, :, pl.ds(128 * i, 128)], tiles.at[i], target_sem).start()

    def remote(k, slab, piece, who, src, unit):
        window = pl.ds(ROWS * piece, ROWS)
        return pltpu.make_async_remote_copy(
            src_ref=s.at[unit, slab, window] if src is None else src.at[window],
            dst_ref=s.at[k, slab, window],
            send_sem=link_sem.at[unit],
            recv_sem=recv_sem.at[k, slab, piece],
            device_id=who,
            device_id_type=MESH,
        )

    def send(k, slab, piece, who, src=None, unit=None):
        remote(k, slab, piece, who, src, k if unit is None else unit).start()

    def arrived(k, slab, piece):
        remote(k, slab, piece, to_left, None, k).wait_recv()

    def share(k, slab, src=None):
        pltpu.make_async_remote_copy(
            src_ref=s.at[k, slab] if src is None else src,
            dst_ref=s.at[k, slab],
            send_sem=pass_sem.at[k],
            recv_sem=sibling_sem.at[k],
            device_id=to_sibling,
            device_id_type=MESH,
        ).start()

    def group(k, count, send_sem, recv_sem):
        block = s.at[k, pl.ds(0, count)]
        return pltpu.make_async_remote_copy(
            src_ref=block, dst_ref=block, send_sem=send_sem, recv_sem=recv_sem,
            device_id=to_sibling, device_id_type=MESH,
        )

    mine, other = index(x, hi, core), index(x, 1 - hi, core)
    pieces = range(16 // ROWS)

    def other_out(k, some=pieces):
        for piece in some:
            arrived(k, other, piece)
            for who in (to_left, to_right):
                send(k, other, piece, who)
            send(k + 2, other, piece, to_next, unit=k)
        if pieces[-1] in some:
            share(k, other)

    def passed_out(k, half):
        slab = index(x, half, core)
        for piece in pieces:
            arrived(k, slab, piece)
            for who in (to_left, to_right):
                send(k, slab, piece, who)
        share(k, slab)

    def sides(k, half):
        from_left, from_right = index(left, half, core), index(right_x, half, core)

        def relay(piece):
            if piece < len(pieces) // 2:
                send(k, from_left, piece, to_right)
            else:
                send(k, from_right, piece, to_left)

        for piece in pieces:
            arrived(k, from_left, piece)
            arrived(k, from_right, piece)
            if k < 2:
                relay(piece)
        if k >= 2:
            @pl.when(from_wrap == 1)
            def _():
                for piece in pieces:
                    relay(piece)

        share(k, from_left)
        share(k, from_right)

    def far(k, half):
        slab = index(across, half, core)
        for piece in pieces:
            arrived(k, slab, piece)
        if k < 2:
            @pl.when(to_wrap == 0)
            def _():
                for piece in pieces:
                    send(k + 2, slab, piece, to_next, unit=k)

        share(k, slab)

    def sent(k):
        group(k, 8, pass_sem.at[k], sibling_sem.at[k]).wait_send()
        flag = to_wrap if k < 2 else from_wrap
        for value, count in ((0, 11 if k < 2 else 4), (1, 9 if k < 2 else 6)):
            @pl.when(flag == value)
            def _():
                group(k, count, link_sem.at[k], sibling_sem.at[k]).wait_send()

    def complete(k):
        group(k, 8, pass_sem.at[k], sibling_sem.at[k]).wait_recv()

    def first(k):
        for u in range(8):
            forward_block(u, t, s.at[k], right, forward, wide)

    def second(k):
        for i in range(4):
            middle_block(i // 2, i % 2, wide, middle, inverse, back)

    def third(k, emit=None):
        for u in range(8):
            backward_block(u, s.at[k], back, right, backward, acc, k == 0, emit)

    def emit(v, value):
        for i, tile in enumerate(swapped(value)):
            out[0, :, 128 * (2 * v + i) : 128 * (2 * v + i) + 128] = tile

    pl.semaphore_wait(barrier, 6)
    for k in range(2):
        for piece in pieces:
            send(k, mine, piece, to_z, source_hbm.at[k])
        for piece in pieces:
            for who in (to_left, to_right):
                send(k, mine, piece, who, source_hbm.at[k])
        for piece in pieces:
            send(k + 2, mine, piece, to_next, source_hbm.at[k], unit=k)
    for k in range(2):
        share(k, mine, source_hbm.at[k])
    pltpu.make_async_copy(tiles, tiles, target_sem).wait()
    swap_in(tiles, t)
    for copy in (*loads, *own):
        copy.wait()
    fill_inverse(lanes, rows, inverse)
    sides(0, hi)
    sides(1, hi)
    passed_out(2, hi)
    other_out(0)
    far(0, hi)
    passed_out(3, hi)
    sides(0, 1 - hi)
    far(1, hi)
    sides(2, hi)
    other_out(1)
    sides(3, hi)
    far(0, 1 - hi)
    passed_out(2, 1 - hi)
    complete(0)
    first(0)
    sides(1, 1 - hi)
    passed_out(3, 1 - hi)
    sides(2, 1 - hi)
    second(0)
    far(1, 1 - hi)
    third(0)
    far(2, hi)
    sides(3, 1 - hi)
    complete(1)
    first(1)
    far(2, 1 - hi)
    far(3, hi)
    second(1)
    far(3, 1 - hi)
    third(1)
    complete(2)
    first(2)
    second(2)
    third(2)
    complete(3)
    first(3)
    for k in range(UNITS):
        sent(k)
    second(3)
    third(3, emit)


def body(targets, sources):
    constants = [jnp.asarray(a) for a in tables()]
    slabs = sources.reshape(2, 4, 32, 128).transpose(0, 2, 1, 3).reshape(2, 16, 8, 128)
    anywhere = pl.BlockSpec(memory_space=pl.ANY)
    vmem, dma = pltpu.VMEM, pltpu.SemaphoreType.DMA
    return pl.pallas_call(
        kernel,
        out_shape=vmem((1, 64, 4096), f32),
        in_specs=[anywhere] * 8,
        out_specs=pl.BlockSpec(memory_space=vmem),
        scratch_shapes=[
            vmem((32, 64, 128), f32), vmem((16, 16, 8, 128), f32), vmem((16, 16, 8, 128), f32),
            vmem((UNITS, 16, 16, 8, 128), f32),
            vmem((2, 2, 512, 256), bf16), vmem((2, 2, 256, 256), f32), vmem((2, 2, 256, 256), f32),
            *[vmem(a.shape, a.dtype) for a in constants],
            dma((UNITS,)), dma((UNITS,)), dma((UNITS, 16, 16 // ROWS)), dma((UNITS,)),
            dma((2,)), dma((6,)), dma,
        ],
        compiler_params=pltpu.CompilerParams(
            collective_id=0, has_side_effects=True, vmem_limit_bytes=65900000
        ),
        name="exchange",
    )(targets, slabs, *constants)


def solution(mesh):
    return jax.shard_map(
        body,
        mesh=mesh,
        in_specs=(P(("band", "member"), None, None), P("band", "member", None)),
        out_specs=P(("band", "member"), None, None),
        check_vma=False,
    )
```
